32 devices in a mesh: dp: 4 (over z), mp: 8 (over y, x, core).
Axes of the slice: x: 2, y: 2, z: 4, core: 2. Of those that a mesh axis runs over, the one named last changes fastest.
Arguments:
- gradients: bfloat16 [4, 2, 768, 2048], P('dp', None, None, 'mp'), may hold values from -4 to 4
- weights: bfloat16 [2, 768, 2048], P(None, None, 'mp'), may hold values from -4 to 4
- projection: float32 [2, 768, 256], replicated, may hold values from -0.21875 to 0.21875
- moment_first: float32 [2, 256, 2048], P(None, 'dp', 'mp'), may hold values from -6 to 6
- moment_second: float32 [2, 256, 2048], P(None, 'dp', 'mp'), may hold values from 0.25 to 4
Outputs:
- new_weights: bfloat16 [2, 768, 2048], P(None, None, 'mp')
- new_first: float32 [2, 256, 2048], P(None, 'dp', 'mp')
- new_second: float32 [2, 256, 2048], P(None, 'dp', 'mp')
- new_bases: float32 [2, 768, 256], replicated
The draws below stay inside these ranges and needn't reach their ends.
All inputs are finite; a program needn't handle non-finite values.
Results may differ from the reference program's by a relative error of at most 0.0004.
Values may be sent and summed in bfloat16 or wider, within the bound.
A program may use at most 64 MiB of HBM per device.

```python
import math
import jax
import jax.numpy as jnp
from jax import lax

D = 768
F = 2048
R = 256
L = 2
NS_ITERS = 4
REPLICAS = 4


def block_levels(rng, extent, shards, least, largest):
    def one(position, shards_of):
        draws = jax.random.uniform(jax.random.fold_in(jax.random.fold_in(rng, 6), position), (shards_of,), jnp.float32, least / len(shards), largest / len(shards))
        return jnp.repeat(jnp.exp(draws), extent[position] // shards_of).reshape((-1,) + (1,) * (len(extent) - position - 1))

    loudness = one(*shards[0])
    for cut in shards[1:]:
        loudness = loudness * one(*cut)
    return loudness


def bell_draw(key, shape, deviation, limit, split=(), kind=jnp.bfloat16):
    values = jax.random.normal(key, shape, jnp.float32) * deviation
    if len(split) > 0:
        values = block_levels(key, shape, split, -0.22, 0.18) * values
    return jnp.clip(values, min=-limit, max=limit).astype(kind)


def setup_inputs(seed: int = 0) -> dict:
    arg_keys = jax.random.split(jax.random.key(seed), 6)
    return {
        "gradients": bell_draw(arg_keys[0], (REPLICAS, L, D, F), 0.25, 4.0, ((0, 4), (3, 8))),
        "weights": bell_draw(arg_keys[1], (L, D, F), 0.25, 4.0, ((2, 8),)),
        "projection": bell_draw(arg_keys[2], (L, D, R), D ** -0.5, 0.21875, (), jnp.float32),
        "moment_first": bell_draw(arg_keys[3], (L, R, F), 0.5, 6.0, ((1, 4), (2, 8)), jnp.float32),
        "moment_second": jnp.clip(jnp.exp(math.log(4.0) - 2.7725887 * jax.random.uniform(arg_keys[4], (L, R, F), jnp.float32) ** block_levels(arg_keys[4], (L, R, F), ((1, 4), (2, 8)), -0.2, 0.2)), 0.25, 4.0),
    }


beta_first = 0.5
beta_second = 0.5
adam_eps = 1e-06
learn_rate = 0.1

def newton_schulz(subspace):
    highest = lax.Precision.HIGHEST
    factor = 1.0 / (jnp.sqrt(lax.optimization_barrier(jnp.sum(subspace * subspace, axis=(1, 2), keepdims=True))) + 1e-06)
    current = subspace * factor
    for sweep in range(NS_ITERS):
        gram = jnp.einsum('ldr,lds->lrs', current, current, precision=highest)
        current = 1.5 * current - 0.5 * jnp.einsum('ldr,lrs->lds', current, gram, precision=highest)
    return current

def reference(gradients, weights, projection, moment_first, moment_second):
    highest = lax.Precision.HIGHEST
    summed = lax.optimization_barrier(jnp.sum(gradients.astype(jnp.float32), axis=0))
    lowrank = jnp.einsum('ldr,ldf->lrf', projection, summed, precision=highest)
    new_first = beta_first * moment_first + (1.0 - beta_first) * lowrank
    new_second = beta_second * moment_second + (1.0 - beta_second) * lowrank * lowrank
    direction = new_first / (jnp.sqrt(new_second) + adam_eps)
    delta = jnp.einsum('ldr,lrf->ldf', projection, direction, precision=highest)
    new_weights = (weights.astype(jnp.float32) - learn_rate * delta).astype(jnp.bfloat16)
    subspace = jnp.einsum('ldf,lrf->ldr', summed, lowrank, precision=highest)
    new_bases = newton_schulz(subspace)
    return (new_weights, new_first, new_second, new_bases)
```

```python
import functools

import jax
import jax.numpy as jnp
from jax import lax
from jax.experimental import pallas as pl
from jax.experimental.pallas import tpu as pltpu
from jax.sharding import PartitionSpec as P

NS_ITERS = 4
CORES = 2
LANES = 128
SUBLANES = 8

beta_first = 0.5
beta_second = 0.5
adam_eps = 1e-06
learn_rate = 0.1

MESH = pl.DeviceIdType.MESH
NN = (((1,), (0,)), ((), ()))
NT = (((1,), (1,)), ((), ()))
TN = (((0,), (0,)), ((), ()))


def split(value):
    high = value.astype(jnp.bfloat16)
    low = (value - high.astype(jnp.float32)).astype(jnp.bfloat16)
    return high, low


def product(a, b, dims=NN):
    dot = functools.partial(lax.dot_general, dimension_numbers=dims, preferred_element_type=jnp.float32)
    return dot(a[0], b[0]) + (dot(a[0], b[1]) + dot(a[1], b[0]))


def step_kernel(
    n, q, grad, weight, basis, first, second,
    out_weight, out_first, out_second, out_basis,
    grad_in, basis_v, basis_t, weight_v, first_v, second_v,
    low_v, low_in, dir_all, part, plane_in, z_out, z_in, sub,
    new_weight, new_first, new_second, new_basis,
    load_sem, store_sem,
    grad_send, grad_recv, low_send, low_recv, dir_send, dir_recv,
    plane_send, plane_recv, z_send, z_recv, sub_send, sub_recv, base_send, base_recv,
):
    z = lax.axis_index("dp")
    mp = lax.axis_index("mp")
    core, plane = lax.rem(mp, CORES), lax.div(mp, CORES)
    half = n // CORES
    width = low_v.shape[1]
    rank_rows = first.shape[1]
    z_peer = [lax.rem(z + d, n) for d in range(n)]
    plane_peer = [lax.rem(plane + d, q) for d in range(q)]

    def device(z_at, plane_at, core_at):
        return (z_at, plane_at * CORES + core_at)

    def remote(src, dst, send, recv, target):
        return pltpu.make_async_remote_copy(
            src_ref=src, dst_ref=dst, send_sem=send, recv_sem=recv, device_id=target, device_id_type=MESH
        )

    def arrived(ref, recv):
        pltpu.make_async_copy(ref, ref, recv).wait()

    loads = [
        pltpu.make_async_copy(src, dst, load_sem.at[at])
        for at, (src, dst) in enumerate(
            ((basis, basis_v), (first, first_v), (second, second_v), (weight, weight_v))
        )
    ]
    for load in loads:
        load.start()

    barrier = pltpu.get_barrier_semaphore()
    for d in range(n):
        for c in range(CORES):
            if d + c > 0:
                target = device(z_peer[d], plane, lax.rem(core + c, CORES))
                pl.semaphore_signal(barrier, inc=1, device_id=target, device_id_type=MESH)
    for d in range(1, q):
        pl.semaphore_signal(barrier, inc=1, device_id=device(z, plane_peer[d], core), device_id_type=MESH)
    pl.semaphore_wait(barrier, n * CORES - 1 + q - 1)

    grad_sends = []
    for layer in range(CORES):
        for s in range(half):
            owner = core * half + s
            src = grad.at[0, layer, :, pl.ds(s * width, width)]
            own = jnp.logical_and(owner == z, core == layer)
            send = remote(
                src, grad_in.at[z], grad_send.at[layer, s], grad_recv.at[z], device(owner, plane, layer)
            )

            @pl.when(own)
            def _(src=src):
                pltpu.make_async_copy(src, grad_in.at[z], grad_recv.at[z]).start()

            @pl.when(jnp.logical_not(own))
            def _(send=send):
                send.start()

            grad_sends.append((own, send))

    loads[0].wait()
    t_high, t_low = split(basis_v[core].T)
    basis_t[0] = t_high
    basis_t[1] = t_low

    for d in range(n):
        arrived(grad_in.at[z_peer[d]], grad_recv.at[z_peer[d]])
    total = grad_in[0].astype(jnp.float32)
    for r in range(1, n):
        total = total + grad_in[r].astype(jnp.float32)
    total = split(total)
    low = product((basis_t[0], basis_t[1]), total)
    low_v[...] = low

    column_core, column_slot = lax.div(z, half), lax.rem(z, half)
    low_sends = []
    for d in range(n):
        src = low_v.at[pl.ds(pl.multiple_of(z_peer[d] * rank_rows, SUBLANES), rank_rows), :]
        dst = low_in.at[core, column_slot]
        recv = low_recv.at[core, column_slot]
        send = remote(src, dst, low_send.at[d], recv, device(z_peer[d], plane, column_core))
        if d > 0:
            send.start()
            low_sends.append((None, send))
        else:
            own = column_core == core

            @pl.when(own)
            def _(src=src, dst=dst, recv=recv):
                pltpu.make_async_copy(src, dst, recv).start()

            @pl.when(jnp.logical_not(own))
            def _(send=send):
                send.start()

            low_sends.append((own, send))

    part[...] = product(total, split(low), NT).reshape(part.shape)
    plain_sends = []
    for e in list(range(1, n)) + [0]:
        for d in range(1, q):
            send = remote(
                part.at[plane_peer[d], z_peer[e]], plane_in.at[plane, z_peer[e]],
                plane_send.at[d, e], plane_recv.at[plane, z_peer[e]], device(z, plane_peer[d], core),
            )
            send.start()
            plain_sends.append(send)

    for layer in range(CORES):
        for s in range(half):
            arrived(low_in.at[layer, s], low_recv.at[layer, s])
    loads[1].wait()
    loads[2].wait()
    for layer in range(CORES):
        for s in range(half):
            columns = pl.ds(s * width, width)
            mine = low_in[layer, s]
            moved = beta_first * first_v[layer, :, columns] + (1.0 - beta_first) * mine
            spread = beta_second * second_v[layer, :, columns] + (1.0 - beta_second) * mine * mine
            new_first[layer, :, columns] = moved
            new_second[layer, :, columns] = spread
            dir_all[z, layer, :, columns] = moved / (jnp.sqrt(spread) + adam_eps)
    for d in range(1, n):
        send = remote(
            dir_all.at[z], dir_all.at[z], dir_send.at[d], dir_recv.at[z], device(z_peer[d], plane, core)
        )
        send.start()
        plain_sends.append(send)
    stores = [
        pltpu.make_async_copy(new_first, out_first, store_sem.at[0]),
        pltpu.make_async_copy(new_second, out_second, store_sem.at[1]),
    ]
    for store in stores:
        store.start()

    def plane_sum(e):
        for d in range(1, q):
            arrived(plane_in.at[plane_peer[d], z_peer[e]], plane_recv.at[plane_peer[d], z_peer[e]])
        value = part[plane, z_peer[e]]
        for d in range(1, q):
            value = value + plane_in[plane_peer[d], z_peer[e]]
        return value

    for e in range(1, n):
        z_out[e] = plane_sum(e)
        send = remote(
            z_out.at[e], z_in.at[z], z_send.at[e], z_recv.at[z], device(z_peer[e], plane, core)
        )
        send.start()
        plain_sends.append(send)
    value = plane_sum(0)
    for e in range(1, n):
        arrived(z_in.at[z_peer[e]], z_recv.at[z_peer[e]])
    for e in range(1, n):
        value = value + z_in[z_peer[e]]
    sub[plane, z] = value

    def spread_plane(e):
        for d in range(1, q):
            block = sub.at[plane, z_peer[e]]
            send = remote(
                block, block, sub_send.at[d, e], sub_recv.at[plane, z_peer[e]], device(z, plane_peer[d], core)
            )
            send.start()
            plain_sends.append(send)

    for e in range(1, n):
        block = sub.at[plane, z]
        send = remote(block, block, sub_send.at[0, e], sub_recv.at[plane, z], device(z_peer[e], plane, core))
        send.start()
        plain_sends.append(send)
    spread_plane(0)

    for d in range(1, n):
        arrived(dir_all.at[z_peer[d]], dir_recv.at[z_peer[d]])
    loads[3].wait()

    def update(layer):
        direction = dir_all[:, layer].reshape(n * rank_rows, dir_all.shape[3])
        delta = product(split(basis_v[layer]), split(direction))
        new_weight[layer] = (weight_v[layer].astype(jnp.float32) - learn_rate * delta).astype(jnp.bfloat16)

    update(0)
    for e in range(1, n):
        arrived(sub.at[plane, z_peer[e]], sub_recv.at[plane, z_peer[e]])
        spread_plane(e)
    update(1)
    store = pltpu.make_async_copy(new_weight, out_weight, store_sem.at[2])
    store.start()
    stores.append(store)

    for e in range(n):
        for d in range(1, q):
            arrived(sub.at[plane_peer[d], z_peer[e]], sub_recv.at[plane_peer[d], z_peer[e]])

    depth, rank = new_basis.shape
    current = sub[...].reshape(depth, rank)
    current = current * (1.0 / (jnp.sqrt(jnp.sum(current * current)) + 1e-06))
    start = split(current)
    gram = product(start, start, TN)
    rows = lax.broadcasted_iota(jnp.int32, (rank, rank), 0)
    columns = lax.broadcasted_iota(jnp.int32, (rank, rank), 1)
    scaled_eye = jnp.where(rows == columns, 1.5, 0.0)
    chain = None
    for sweep in range(NS_ITERS):
        factor = scaled_eye - 0.5 * gram
        pieces = split(factor)
        chain = factor if chain is None else product(split(chain), pieces)
        if sweep < NS_ITERS - 1:
            gram = product(pieces, split(product(split(gram), pieces)))
    chain = split(chain)
    chunk = depth // q
    base_copies = []
    for at in range(q):
        span = pl.ds(at * chunk, chunk)
        lines = slice(at * chunk, (at + 1) * chunk)
        new_basis[span, :] = product((start[0][lines], start[1][lines]), chain)
        send = remote(
            new_basis.at[span, :], out_basis.at[core, span, :], base_send.at[at], base_recv.at[at],
            device(z, plane, 1 - core),
        )
        send.start()
        plain_sends.append(send)
        store = pltpu.make_async_copy(new_basis.at[span, :], out_basis.at[core, span, :], store_sem.at[3 + at])
        store.start()
        stores.append(store)

    for own, send in grad_sends + low_sends:
        if own is None:
            send.wait_send()
        else:
            @pl.when(jnp.logical_not(own))
            def _(send=send):
                send.wait_send()
    for send in plain_sends:
        send.wait_send()
    for at in range(q):
        block = out_basis.at[1 - core, pl.ds(at * chunk, chunk), :]
        arrived(block, base_recv.at[at])
    for store in stores:
        store.wait()


def fused_step(gradients, weights, projection, moment_first, moment_second):
    n = lax.axis_size("dp")
    q = lax.axis_size("mp") // CORES
    layers, depth, columns = weights.shape
    rank = projection.shape[2]
    rank_rows = moment_first.shape[1]
    half = n // CORES
    width = columns // half
    piece = depth // (q * n)
    f32, bf16 = jnp.float32, jnp.bfloat16
    dma = pltpu.SemaphoreType.DMA
    anywhere = pl.BlockSpec(memory_space=pl.ANY)
    outs = pl.pallas_call(
        functools.partial(step_kernel, n, q),
        name="galore_step",
        out_shape=(
            jax.ShapeDtypeStruct(weights.shape, bf16),
            jax.ShapeDtypeStruct(moment_first.shape, f32),
            jax.ShapeDtypeStruct(moment_second.shape, f32),
            jax.ShapeDtypeStruct(projection.shape, f32),
        ),
        in_specs=[anywhere] * 5,
        out_specs=(anywhere,) * 4,
        scratch_shapes=[
            pltpu.VMEM((n, depth, width), bf16),
            pltpu.VMEM(projection.shape, f32),
            pltpu.VMEM((2, rank, depth), bf16),
            pltpu.VMEM(weights.shape, bf16),
            pltpu.VMEM(moment_first.shape, f32),
            pltpu.VMEM(moment_second.shape, f32),
            pltpu.VMEM((rank, width), f32),
            pltpu.VMEM((CORES, half, rank_rows, width), f32),
            pltpu.VMEM((n, layers, rank_rows, columns), f32),
            pltpu.VMEM((q, n, piece, rank), f32),
            pltpu.VMEM((q, n, piece, rank), f32),
            pltpu.VMEM((n, piece, rank), f32),
            pltpu.VMEM((n, piece, rank), f32),
            pltpu.VMEM((q, n, piece, rank), f32),
            pltpu.VMEM(weights.shape, bf16),
            pltpu.VMEM(moment_first.shape, f32),
            pltpu.VMEM(moment_second.shape, f32),
            pltpu.VMEM((depth, rank), f32),
            dma((4,)),
            dma((3 + q,)),
            dma((CORES, half)),
            dma((n,)),
            dma((n,)),
            dma((CORES, half)),
            dma((n,)),
            dma((n,)),
            dma((q, n)),
            dma((q, n)),
            dma((n,)),
            dma((n,)),
            dma((q, n)),
            dma((q, n)),
            dma((q,)),
            dma((q,)),
        ],
        compiler_params=pltpu.CompilerParams(collective_id=0, has_side_effects=True),
    )(gradients, weights, projection, moment_first, moment_second)
    return tuple(outs)


def newton_schulz(subspace):
    highest = lax.Precision.HIGHEST
    factor = 1.0 / (jnp.sqrt(jnp.sum(subspace * subspace, axis=(1, 2), keepdims=True)) + 1e-06)
    current = subspace * factor
    for sweep in range(NS_ITERS):
        gram = jnp.einsum("ldr,lds->lrs", current, current, precision=highest)
        current = 1.5 * current - 0.5 * jnp.einsum("ldr,lrs->lds", current, gram, precision=highest)
    return current


def back_project(bases_rows, direction_own):
    highest = lax.Precision.HIGHEST
    return jnp.einsum(
        "ldr,lrf->ldf",
        bases_rows,
        lax.all_gather(direction_own, "dp", axis=1, tiled=True),
        precision=highest,
    )


def plain_step(gradients, weights, projection, moment_first, moment_second):
    highest = lax.Precision.HIGHEST
    local_grad = gradients[0].astype(jnp.float32)
    totals = lax.psum(local_grad, "dp")
    lowrank = jnp.einsum("ldr,ldf->lrf", projection, totals, precision=highest)
    partial_sub = jnp.einsum("ldf,lrf->ldr", totals, lowrank, precision=highest)
    subspace = lax.psum(partial_sub, "mp")
    rank_rows = moment_first.shape[1]
    rank_start = lax.axis_index("dp") * rank_rows
    low_own = lax.dynamic_slice_in_dim(lowrank, rank_start, rank_rows, 1)
    new_first = beta_first * moment_first + (1.0 - beta_first) * low_own
    new_second = beta_second * moment_second + (1.0 - beta_second) * low_own * low_own
    direction_own = new_first / (jnp.sqrt(new_second) + adam_eps)
    width_rows = weights.shape[1] // lax.axis_size("dp")
    row_start = lax.axis_index("dp") * width_rows
    bases_rows = lax.dynamic_slice_in_dim(projection, row_start, width_rows, 1)
    weight_rows = lax.dynamic_slice_in_dim(weights, row_start, width_rows, 1)
    delta_rows = back_project(bases_rows, direction_own)
    updated = (weight_rows.astype(jnp.float32) - learn_rate * delta_rows).astype(jnp.bfloat16)
    new_weights = lax.all_gather(updated, "dp", axis=1, tiled=True)
    new_bases = newton_schulz(subspace)
    return (new_weights, new_first, new_second, new_bases)


def shards(gradients, weights, projection, moment_first, moment_second):
    n = lax.axis_size("dp")
    q = lax.axis_size("mp") // CORES
    layers, depth, columns = weights.shape
    rank_rows = moment_first.shape[1]
    whole_tiles = (
        layers == CORES
        and gradients.shape[0] == 1
        and n % CORES == 0
        and columns % (n // CORES * LANES) == 0
        and depth % (q * n * SUBLANES) == 0
        and rank_rows % SUBLANES == 0
    )
    step = fused_step if whole_tiles else plain_step
    return step(gradients, weights, projection, moment_first, moment_second)


def solution(mesh):
    placed = (
        P("dp", None, None, "mp"),
        P(None, None, "mp"),
        P(),
        P(None, "dp", "mp"),
        P(None, "dp", "mp"),
    )
    return jax.shard_map(
        shards,
        mesh=mesh,
        in_specs=placed,
        out_specs=(P(None, None, "mp"), P(None, "dp", "mp"), P(None, "dp", "mp"), P()),
        check_vma=False,
    )
```

```python
import functools

import jax
import jax.numpy as jnp
from jax import lax
from jax.experimental import pallas as pl
from jax.experimental.pallas import tpu as pltpu
from jax.sharding import PartitionSpec as P

NS_ITERS = 4
CORES = 2
LANES = 128
SUBLANES = 8

beta_first = 0.5
beta_second = 0.5
adam_eps = 1e-06
learn_rate = 0.1

MESH = pl.DeviceIdType.MESH
NN = (((1,), (0,)), ((), ()))
NT = (((1,), (1,)), ((), ()))
TN = (((0,), (0,)), ((), ()))


def split(value):
    high = value.astype(jnp.bfloat16)
    low = (value - high.astype(jnp.float32)).astype(jnp.bfloat16)
    return high, low


def product(a, b, dims=NN):
    dot = functools.partial(lax.dot_general, dimension_numbers=dims, preferred_element_type=jnp.float32)
    return dot(a[0], b[0]) + (dot(a[0], b[1]) + dot(a[1], b[0]))


def step_kernel(
    n, q, grad, weight, basis, first, second,
    out_weight, out_first, out_second, out_basis,
    grad_in, basis_v, basis_t, weight_v, first_v, second_v,
    low_v, low_in, dir_all, part, plane_in, z_out, z_in, sub,
    new_weight, new_first, new_second, new_basis,
    load_sem, store_sem, weight_sem,
    grad_send, grad_recv, low_send, low_recv, dir_send, dir_recv,
    plane_send, plane_recv, z_send, z_recv, sub_send, sub_recv, base_send, base_recv,
):
    z = lax.axis_index("dp")
    mp = lax.axis_index("mp")
    core, plane = lax.rem(mp, CORES), lax.div(mp, CORES)
    half = n // CORES
    width = low_v.shape[1]
    rank_rows = first.shape[1]
    z_peer = [lax.rem(z + d, n) for d in range(n)]
    plane_peer = [lax.rem(plane + d, q) for d in range(q)]

    def device(z_at, plane_at, core_at):
        return (z_at, plane_at * CORES + core_at)

    def remote(src, dst, send, recv, target):
        return pltpu.make_async_remote_copy(
            src_ref=src, dst_ref=dst, send_sem=send, recv_sem=recv, device_id=target, device_id_type=MESH
        )

    def arrived(ref, recv):
        pltpu.make_async_copy(ref, ref, recv).wait()

    loads = [
        pltpu.make_async_copy(src, dst, load_sem.at[at])
        for at, (src, dst) in enumerate(
            ((basis, basis_v), (first, first_v), (second, second_v), (weight, weight_v))
        )
    ]
    for load in loads:
        load.start()

    barrier = pltpu.get_barrier_semaphore()
    for d in range(n):
        for c in range(CORES):
            if d + c > 0:
                target = device(z_peer[d], plane, lax.rem(core + c, CORES))
                pl.semaphore_signal(barrier, inc=1, device_id=target, device_id_type=MESH)
    for d in range(1, q):
        pl.semaphore_signal(barrier, inc=1, device_id=device(z, plane_peer[d], core), device_id_type=MESH)
    pl.semaphore_wait(barrier, n * CORES - 1 + q - 1)

    grad_sends = []
    for layer in range(CORES):
        for s in range(half):
            owner = core * half + s
            src = grad.at[0, layer, :, pl.ds(s * width, width)]
            own = jnp.logical_and(owner == z, core == layer)
            send = remote(
                src, grad_in.at[z], grad_send.at[layer, s], grad_recv.at[z], device(owner, plane, layer)
            )

            @pl.when(own)
            def _(src=src):
                pltpu.make_async_copy(src, grad_in.at[z], grad_recv.at[z]).start()

            @pl.when(jnp.logical_not(own))
            def _(send=send):
                send.start()

            grad_sends.append((own, send))

    loads[0].wait()
    t_high, t_low = split(basis_v[core].T)
    basis_t[0] = t_high
    basis_t[1] = t_low

    for d in range(n):
        arrived(grad_in.at[z_peer[d]], grad_recv.at[z_peer[d]])
    total = grad_in[0].astype(jnp.float32)
    for r in range(1, n):
        total = total + grad_in[r].astype(jnp.float32)
    total = split(total)
    low = product((basis_t[0], basis_t[1]), total)
    low_v[...] = low

    column_core, column_slot = lax.div(z, half), lax.rem(z, half)
    low_sends = []
    for d in range(n):
        src = low_v.at[pl.ds(pl.multiple_of(z_peer[d] * rank_rows, SUBLANES), rank_rows), :]
        dst = low_in.at[core, column_slot]
        recv = low_recv.at[core, column_slot]
        send = remote(src, dst, low_send.at[d], recv, device(z_peer[d], plane, column_core))
        if d > 0:
            send.start()
            low_sends.append((None, send))
        else:
            own = column_core == core

            @pl.when(own)
            def _(src=src, dst=dst, recv=recv):
                pltpu.make_async_copy(src, dst, recv).start()

            @pl.when(jnp.logical_not(own))
            def _(send=send):
                send.start()

            low_sends.append((own, send))

    part[...] = product(total, split(low), NT).reshape(part.shape)
    plain_sends = []
    for e in list(range(1, n)) + [0]:
        for d in range(1, q):
            send = remote(
                part.at[plane_peer[d], z_peer[e]], plane_in.at[plane, z_peer[e]],
                plane_send.at[d, e], plane_recv.at[plane, z_peer[e]], device(z, plane_peer[d], core),
            )
            send.start()
            plain_sends.append(send)

    for layer in range(CORES):
        for s in range(half):
            arrived(low_in.at[layer, s], low_recv.at[layer, s])
    loads[1].wait()
    loads[2].wait()
    for layer in range(CORES):
        for s in range(half):
            columns = pl.ds(s * width, width)
            mine = low_in[layer, s]
            moved = beta_first * first_v[layer, :, columns] + (1.0 - beta_first) * mine
            spread = beta_second * second_v[layer, :, columns] + (1.0 - beta_second) * mine * mine
            new_first[layer, :, columns] = moved
            new_second[layer, :, columns] = spread
            dir_all[z, layer, :, columns] = moved / (jnp.sqrt(spread) + adam_eps)
    stores = [
        pltpu.make_async_copy(new_first, out_first, store_sem.at[0]),
        pltpu.make_async_copy(new_second, out_second, store_sem.at[1]),
    ]
    for store in stores:
        store.start()

    def plane_sum(e):
        for d in range(1, q):
            arrived(plane_in.at[plane_peer[d], z_peer[e]], plane_recv.at[plane_peer[d], z_peer[e]])
        value = part[plane, z_peer[e]]
        for d in range(1, q):
            value = value + plane_in[plane_peer[d], z_peer[e]]
        return value

    for e in range(1, n):
        z_out[e] = plane_sum(e)
        send = remote(
            z_out.at[e], z_in.at[z], z_send.at[e], z_recv.at[z], device(z_peer[e], plane, core)
        )
        send.start()
        plain_sends.append(send)
    value = plane_sum(0)
    for e in range(1, n):
        arrived(z_in.at[z_peer[e]], z_recv.at[z_peer[e]])
    for e in range(1, n):
        value = value + z_in[z_peer[e]]
    sub[plane, z] = value

    def spread_plane(e):
        for d in range(1, q):
            block = sub.at[plane, z_peer[e]]
            send = remote(
                block, block, sub_send.at[d, e], sub_recv.at[plane, z_peer[e]], device(z, plane_peer[d], core)
            )
            send.start()
            plain_sends.append(send)

    for e in range(1, n):
        block = sub.at[plane, z]
        send = remote(block, block, sub_send.at[0, e], sub_recv.at[plane, z], device(z_peer[e], plane, core))
        send.start()
        plain_sends.append(send)
    spread_plane(0)

    for d in range(1, n):
        send = remote(
            dir_all.at[z], dir_all.at[z], dir_send.at[d], dir_recv.at[z], device(z_peer[d], plane, core)
        )
        send.start()
        plain_sends.append(send)
    for e in range(1, n):
        arrived(sub.at[plane, z_peer[e]], sub_recv.at[plane, z_peer[e]])
        spread_plane(e)

    for e in range(n):
        for d in range(1, q):
            arrived(sub.at[plane_peer[d], z_peer[e]], sub_recv.at[plane_peer[d], z_peer[e]])

    depth, rank = new_basis.shape
    current = sub[...].reshape(depth, rank)
    current = current * (1.0 / (jnp.sqrt(jnp.sum(current * current)) + 1e-06))
    start = split(current)
    gram = product(start, start, TN)
    rows = lax.broadcasted_iota(jnp.int32, (rank, rank), 0)
    columns = lax.broadcasted_iota(jnp.int32, (rank, rank), 1)
    scaled_eye = jnp.where(rows == columns, 1.5, 0.0)
    chain = None
    for sweep in range(NS_ITERS):
        factor = scaled_eye - 0.5 * gram
        pieces = split(factor)
        chain = factor if chain is None else product(split(chain), pieces)
        if sweep < NS_ITERS - 1:
            gram = product(pieces, split(product(split(gram), pieces)))
    chain = split(chain)
    chunk = depth // q
    base_copies = []
    for at in range(q):
        span = pl.ds(at * chunk, chunk)
        lines = slice(at * chunk, (at + 1) * chunk)
        new_basis[span, :] = product((start[0][lines], start[1][lines]), chain)
        send = remote(
            new_basis.at[span, :], out_basis.at[core, span, :], base_send.at[at], base_recv.at[at],
            device(z, plane, 1 - core),
        )
        send.start()
        plain_sends.append(send)
        store = pltpu.make_async_copy(new_basis.at[span, :], out_basis.at[core, span, :], store_sem.at[3 + at])
        store.start()
        stores.append(store)

    for d in range(1, n):
        arrived(dir_all.at[z_peer[d]], dir_recv.at[z_peer[d]])
    loads[3].wait()
    for layer in range(CORES):
        direction = dir_all[:, layer].reshape(n * rank_rows, dir_all.shape[3])
        delta = product(split(basis_v[layer]), split(direction))
        new_weight[layer] = (weight_v[layer].astype(jnp.float32) - learn_rate * delta).astype(jnp.bfloat16)
        store = pltpu.make_async_copy(new_weight.at[layer], out_weight.at[layer], weight_sem.at[layer])
        store.start()
        stores.append(store)

    for own, send in grad_sends + low_sends:
        if own is None:
            send.wait_send()
        else:
            @pl.when(jnp.logical_not(own))
            def _(send=send):
                send.wait_send()
    for send in plain_sends:
        send.wait_send()
    for at in range(q):
        block = out_basis.at[1 - core, pl.ds(at * chunk, chunk), :]
        arrived(block, base_recv.at[at])
    for store in stores:
        store.wait()


def pass_kernel(weight, first, second, basis, out_weight, out_first, out_second, out_basis,
                weight_v, first_v, second_v, basis_v, read_sem, write_sem):
    layers = basis.shape[0]
    depth = basis.shape[1] // 2
    parts = []
    for layer in range(layers):
        for at in range(2):
            span = pl.ds(at * depth, depth)
            parts.append(tuple(ref.at[layer, span, :] for ref in (basis, basis_v, out_basis)))
        for refs in ((weight, weight_v, out_weight), (first, first_v, out_first), (second, second_v, out_second)):
            parts.append(tuple(ref.at[layer] for ref in refs))
    reads = [pltpu.make_async_copy(src, mid, read_sem.at[at]) for at, (src, mid, _) in enumerate(parts)]
    writes = [pltpu.make_async_copy(mid, dst, write_sem.at[at]) for at, (_, mid, dst) in enumerate(parts)]
    for read in reads:
        read.start()
    for read, write in zip(reads, writes):
        read.wait()
        write.start()
    for write in writes:
        write.wait()


def pass_on(*arrays):
    anywhere = pl.BlockSpec(memory_space=pl.ANY)
    count = 5 * arrays[3].shape[0]
    return pl.pallas_call(
        pass_kernel,
        name="pass_on",
        out_shape=tuple(jax.ShapeDtypeStruct(a.shape, a.dtype) for a in arrays),
        in_specs=[anywhere] * 4,
        out_specs=(anywhere,) * 4,
        scratch_shapes=[pltpu.VMEM(a.shape, a.dtype) for a in arrays]
        + [pltpu.SemaphoreType.DMA((count,)), pltpu.SemaphoreType.DMA((count,))],
    )(*arrays)


def fused_step(gradients, weights, projection, moment_first, moment_second):
    n = lax.axis_size("dp")
    q = lax.axis_size("mp") // CORES
    layers, depth, columns = weights.shape
    rank = projection.shape[2]
    rank_rows = moment_first.shape[1]
    half = n // CORES
    width = columns // half
    piece = depth // (q * n)
    f32, bf16 = jnp.float32, jnp.bfloat16
    dma = pltpu.SemaphoreType.DMA
    anywhere = pl.BlockSpec(memory_space=pl.ANY)
    outs = pl.pallas_call(
        functools.partial(step_kernel, n, q),
        name="galore_step",
        out_shape=(
            jax.ShapeDtypeStruct(weights.shape, bf16),
            jax.ShapeDtypeStruct(moment_first.shape, f32),
            jax.ShapeDtypeStruct(moment_second.shape, f32),
            jax.ShapeDtypeStruct(projection.shape, f32),
        ),
        in_specs=[anywhere] * 5,
        out_specs=(anywhere,) * 4,
        scratch_shapes=[
            pltpu.VMEM((n, depth, width), bf16),
            pltpu.VMEM(projection.shape, f32),
            pltpu.VMEM((2, rank, depth), bf16),
            pltpu.VMEM(weights.shape, bf16),
            pltpu.VMEM(moment_first.shape, f32),
            pltpu.VMEM(moment_second.shape, f32),
            pltpu.VMEM((rank, width), f32),
            pltpu.VMEM((CORES, half, rank_rows, width), f32),
            pltpu.VMEM((n, layers, rank_rows, columns), f32),
            pltpu.VMEM((q, n, piece, rank), f32),
            pltpu.VMEM((q, n, piece, rank), f32),
            pltpu.VMEM((n, piece, rank), f32),
            pltpu.VMEM((n, piece, rank), f32),
            pltpu.VMEM((q, n, piece, rank), f32),
            pltpu.VMEM(weights.shape, bf16),
            pltpu.VMEM(moment_first.shape, f32),
            pltpu.VMEM(moment_second.shape, f32),
            pltpu.VMEM((depth, rank), f32),
            dma((4,)),
            dma((3 + q,)),
            dma((CORES,)),
            dma((CORES, half)),
            dma((n,)),
            dma((n,)),
            dma((CORES, half)),
            dma((n,)),
            dma((n,)),
            dma((q, n)),
            dma((q, n)),
            dma((n,)),
            dma((n,)),
            dma((q, n)),
            dma((q, n)),
            dma((q,)),
            dma((q,)),
        ],
        compiler_params=pltpu.CompilerParams(collective_id=0, has_side_effects=True),
    )(gradients, weights, projection, moment_first, moment_second)
    return pass_on(*outs)


def newton_schulz(subspace):
    highest = lax.Precision.HIGHEST
    factor = 1.0 / (jnp.sqrt(jnp.sum(subspace * subspace, axis=(1, 2), keepdims=True)) + 1e-06)
    current = subspace * factor
    for sweep in range(NS_ITERS):
        gram = jnp.einsum("ldr,lds->lrs", current, current, precision=highest)
        current = 1.5 * current - 0.5 * jnp.einsum("ldr,lrs->lds", current, gram, precision=highest)
    return current


def back_project(bases_rows, direction_own):
    highest = lax.Precision.HIGHEST
    return jnp.einsum(
        "ldr,lrf->ldf",
        bases_rows,
        lax.all_gather(direction_own, "dp", axis=1, tiled=True),
        precision=highest,
    )


def plain_step(gradients, weights, projection, moment_first, moment_second):
    highest = lax.Precision.HIGHEST
    local_grad = gradients[0].astype(jnp.float32)
    totals = lax.psum(local_grad, "dp")
    lowrank = jnp.einsum("ldr,ldf->lrf", projection, totals, precision=highest)
    partial_sub = jnp.einsum("ldf,lrf->ldr", totals, lowrank, precision=highest)
    subspace = lax.psum(partial_sub, "mp")
    rank_rows = moment_first.shape[1]
    rank_start = lax.axis_index("dp") * rank_rows
    low_own = lax.dynamic_slice_in_dim(lowrank, rank_start, rank_rows, 1)
    new_first = beta_first * moment_first + (1.0 - beta_first) * low_own
    new_second = beta_second * moment_second + (1.0 - beta_second) * low_own * low_own
    direction_own = new_first / (jnp.sqrt(new_second) + adam_eps)
    width_rows = weights.shape[1] // lax.axis_size("dp")
    row_start = lax.axis_index("dp") * width_rows
    bases_rows = lax.dynamic_slice_in_dim(projection, row_start, width_rows, 1)
    weight_rows = lax.dynamic_slice_in_dim(weights, row_start, width_rows, 1)
    delta_rows = back_project(bases_rows, direction_own)
    updated = (weight_rows.astype(jnp.float32) - learn_rate * delta_rows).astype(jnp.bfloat16)
    new_weights = lax.all_gather(updated, "dp", axis=1, tiled=True)
    new_bases = newton_schulz(subspace)
    return (new_weights, new_first, new_second, new_bases)


def shards(gradients, weights, projection, moment_first, moment_second):
    n = lax.axis_size("dp")
    q = lax.axis_size("mp") // CORES
    layers, depth, columns = weights.shape
    rank_rows = moment_first.shape[1]
    whole_tiles = (
        layers == CORES
        and gradients.shape[0] == 1
        and n % CORES == 0
        and columns % (n // CORES * LANES) == 0
        and depth % (q * n * SUBLANES) == 0
        and rank_rows % SUBLANES == 0
    )
    step = fused_step if whole_tiles else plain_step
    return step(gradients, weights, projection, moment_first, moment_second)


def solution(mesh):
    placed = (
        P("dp", None, None, "mp"),
        P(None, None, "mp"),
        P(),
        P(None, "dp", "mp"),
        P(None, "dp", "mp"),
    )
    return jax.shard_map(
        shards,
        mesh=mesh,
        in_specs=placed,
        out_specs=(P(None, None, "mp"), P(None, "dp", "mp"), P(None, "dp", "mp"), P()),
        check_vma=False,
    )
```
